32 devices in a mesh: groups: 2 (over x), hid: 8 (over z, y), wid: 2 (over core).
Axes of the slice: x: 2, y: 2, z: 4, core: 2. Of those that a mesh axis runs over, the one named last changes fastest.
Arguments:
- tokens: bfloat16 [256, 18432], P(('groups', 'hid'), 'wid'), parts along dimension 0, may hold values from -180 to 180
- norm_gain: float32 [18432], P('wid'), may hold values from 0.1 to 1.9
- query_weight: bfloat16 [18432, 8192], P('wid', 'hid'), may hold values from -0.046875 to 0.046875
- query_scale: float32 [8192], P('hid'), may hold values from 0.5 to 2
- kv_weight: bfloat16 [18432, 512], P('wid'), may hold values from -0.046875 to 0.046875
- kv_scale: float32 [512], replicated, may hold values from 0.5 to 2
- keys_cache: bfloat16 [256, 512, 256], P(('groups', 'hid', 'wid')), parts along dimension 0, may hold values from -384 to 384
- values_cache: bfloat16 [256, 512, 256], P(('groups', 'hid', 'wid')), parts along dimension 0, may hold values from -6 to 6
- lengths: int32 [256], P(('groups', 'hid', 'wid')), parts along dimension 0, may hold values from 1 to 512, as said below
Outputs:
- attended: bfloat16 [256, 8192], P(('groups', 'hid', 'wid')), parts along dimension 0
- new_entries: bfloat16 [256, 512], P(('groups', 'hid', 'wid')), parts along dimension 0
The draws below stay inside these ranges and needn't reach their ends.
There are 2 independent parts, one for each index of `groups`. The reference program is written for one: setup_inputs(seed, part) draws one part's arguments, and reference() takes and returns one part's arrays. A program takes and returns all parts, laid end to end along the dimension named above; an argument that names none is the same for every part. Nothing has to cross between parts.
Inputs may be any that keep to these rules, and one draw needn't show every extreme that they name: `lengths`: in one aligned block of 8 requests every length is 512.
All inputs are finite; a program needn't handle non-finite values.
Results may differ from the reference program's by a relative error of at most 0.009.
The reference program's roundings to bfloat16 on the way count: a program that leaves them out, or rounds other values in their place, can miss the bound.
Values may be sent and summed in bfloat16 or wider, within the bound.
A program may use at most 128 MiB of HBM per device.

```python
import math
import jax
import jax.numpy as jnp
from jax import lax

D = 18432
HEADS = 32
HD = 256
REQ_DEV = 8
CACHE = 512
BATCH = 128


def draw_tokens(key, part):
    key_rows, key_cols, key_base = jax.random.split(key, 3)
    row_scale = jnp.exp(jax.random.uniform(key_rows, (BATCH, 1), minval=0.0, maxval=math.log(10.0)))
    col_scale = jnp.exp(jax.random.uniform(key_cols, (1, D), minval=math.log(0.3), maxval=math.log(3.0)))
    base_values = jnp.clip(jax.random.normal(key_base, (BATCH, D)), -6.0, 6.0)
    return (base_values * col_scale * row_scale).astype(jnp.bfloat16)


def draw_keys_cache(key, part):
    key_base = jax.random.fold_in(key, 0)
    base_values = jnp.clip(jax.random.normal(key_base, (BATCH, CACHE, HD)), -6.0, 6.0)
    return base_values.astype(jnp.bfloat16)


def draw_lengths(key, part):
    key_len, key_block = jax.random.split(key)
    drawn_lengths = jax.random.randint(key_len, (BATCH,), 1, CACHE + 1)
    full_block = jax.random.randint(key_block, (), 0, BATCH // REQ_DEV)
    row_block = jnp.arange(BATCH) // REQ_DEV
    return jnp.where(row_block == full_block, CACHE, drawn_lengths).astype(jnp.int32)


def levels(stream_key, shape, cuts, least, high):
    def one(axis_at, parts):
        heights = jax.random.uniform(jax.random.fold_in(jax.random.fold_in(stream_key, 6), axis_at), (parts,), jnp.float32, least / len(cuts), high / len(cuts))
        return jnp.repeat(jnp.exp(heights), shape[axis_at] // parts).reshape((-1,) + (1,) * (len(shape) - axis_at - 1))

    level = one(*cuts[0])
    for cut in cuts[1:]:
        level = level * one(*cut)
    return level


def normal_values(key, extent, spread, reach, shards=(), kind=jnp.bfloat16):
    values = spread * jax.random.normal(key, extent, jnp.float32)
    if shards:
        values = values * levels(key, extent, shards, -0.22, 0.18)
    return jnp.clip(values, -reach, reach).astype(kind)


def setup_inputs(seed: int = 0, part: int = 0) -> dict:
    seeds = jax.random.split(jax.random.key(seed), 10)
    own_keys = jax.random.split(jax.random.fold_in(seeds[9], part), 10)
    return {
        "tokens": draw_tokens(jax.random.fold_in(jax.random.fold_in(seeds[9], part), 71), part),
        "norm_gain": jnp.clip(1.0 + 0.18 * jax.random.normal(seeds[1], (D,), jnp.float32), 0.1, 1.9),
        "query_weight": normal_values(seeds[2], (D, HEADS * HD), D ** -0.5, 0.046875, ((0, 2), (1, 8))),
        "query_scale": jnp.clip(jnp.exp(math.log(2.0) - 1.3862944 * jax.random.uniform(seeds[3], (HEADS * HD,), jnp.float32) ** levels(seeds[3], (HEADS * HD,), ((0, 8),), -0.2, 0.2)), 0.5, 2.0),
        "kv_weight": normal_values(seeds[4], (D, 2 * HD), D ** -0.5, 0.046875, ((0, 2),)),
        "kv_scale": jnp.clip(jnp.exp(jax.random.uniform(seeds[5], (2 * HD,), jnp.float32, math.log(0.5), math.log(2.0))), 0.5, 2.0),
        "keys_cache": draw_keys_cache(jax.random.fold_in(jax.random.fold_in(seeds[9], part), 71), part),
        "values_cache": normal_values(own_keys[7], (BATCH, CACHE, HD), 1.0, 6.0, ((0, 16),)),
        "lengths": draw_lengths(jax.random.fold_in(jax.random.fold_in(seeds[9], part), 71), part),
    }


EPSILON = 1e-05

def attend_all(queries, new_entries, keys_cache, values_cache, lengths):
    row_count, cache_len, head_dim = keys_cache.shape
    head_count = queries.shape[1] // head_dim
    query_heads = queries.reshape(row_count, head_count, head_dim).astype(jnp.float32)
    new_keys = new_entries[:, :head_dim].astype(jnp.float32)
    new_values = new_entries[:, head_dim:].astype(jnp.float32)
    inv_root = head_dim ** (-0.5)
    cache_scores = jnp.einsum('rhd,rtd->rht', query_heads, keys_cache.astype(jnp.float32)) * inv_root
    positions = lax.broadcasted_iota(jnp.int32, (row_count, 1, cache_len), 2)
    is_live = positions < lengths.astype(jnp.int32)[:, None, None]
    cache_scores = jnp.where(is_live, cache_scores, -jnp.inf)
    own_scores = jnp.einsum('rhd,rd->rh', query_heads, new_keys) * inv_root
    peak_score = jnp.maximum(lax.optimization_barrier(jnp.max(cache_scores, axis=2)), own_scores)
    cache_exp = jnp.exp(cache_scores - peak_score[:, :, None])
    own_exp = jnp.exp(own_scores - peak_score)
    denom_sum = lax.optimization_barrier(jnp.sum(cache_exp, axis=2)) + own_exp
    cache_weights = (cache_exp / denom_sum[:, :, None]).astype(jnp.bfloat16)
    own_weights = (own_exp / denom_sum).astype(jnp.bfloat16)
    blended = jnp.einsum('rht,rtd->rhd', cache_weights.astype(jnp.float32), values_cache.astype(jnp.float32))
    blended = blended + own_weights.astype(jnp.float32)[:, :, None] * new_values[:, None, :]
    return blended.reshape(row_count, head_count * head_dim).astype(jnp.bfloat16)

def reference(tokens, norm_gain, query_weight, query_scale, kv_weight, kv_scale, keys_cache, values_cache, lengths):
    row_values = tokens.astype(jnp.float32)
    row_mean = lax.optimization_barrier(jnp.mean(row_values, axis=1))
    variance = lax.optimization_barrier(jnp.mean(row_values * row_values, axis=1)) - row_mean * row_mean
    normed = ((row_values - row_mean[:, None]) * lax.rsqrt(variance + EPSILON)[:, None] * norm_gain.astype(jnp.float32)).astype(jnp.bfloat16)
    queries = (jnp.dot(normed, query_weight, preferred_element_type=jnp.float32) * query_scale.astype(jnp.float32)).astype(jnp.bfloat16)
    new_entries = (jnp.dot(normed, kv_weight, preferred_element_type=jnp.float32) * kv_scale.astype(jnp.float32)).astype(jnp.bfloat16)
    attended = attend_all(queries, new_entries, keys_cache, values_cache, lengths)
    return (attended, new_entries)
```

```python
import functools

import jax
import jax.numpy as jnp
from jax import lax
from jax.experimental import pallas as pl
from jax.experimental.pallas import tpu as pltpu
from jax.sharding import PartitionSpec as P

EPSILON = 1e-05
ROWS_Y = 2
TWELFTHS = (2, 2, 2, 2, 1, 1, 2)
AHEAD = 2
BEHIND = 2
TURN_OWN = 2
TURN_AT = 3
TURN_STEP = 2
UP, DOWN, SIDE = 0, 1, 2
MESH = pl.DeviceIdType.MESH


def kernel(
    hid_count, wid_count,
    tok_hbm, gain_hbm, qw_hbm, qs_hbm, kw_hbm, ks_hbm, keys_hbm, vals_hbm, len_hbm,
    att_ref, new_ref,
    tok, gain, qw, qs, kw, ks, keys, vals, lens,
    gat, stat_mine, stat_other, acc, acc_rx, kv_acc, kv_rx, kv_new,
    q_tx, q_rx, q_f32, o_f32, att,
    in_sem, pair_sem, send_sem, turn_send, line_sem, side_sem, turn_sem,
    acc_send, acc_recv, q_send, q_recv, out_sem,
):
    own_rows, half_width = tok_hbm.shape
    full_width = half_width * wid_count
    unit = half_width // sum(TWELFTHS)
    widths = [t * unit for t in TWELFTHS]
    starts = [sum(widths[:c]) for c in range(len(widths))]
    plain = len(widths) - 1
    turned = plain
    tiles, _, _, req, head_dim = acc.shape
    z_count = hid_count // ROWS_Y
    me = lax.axis_index("hid")
    core = lax.axis_index("wid")
    other = 1 - core
    z = me // ROWS_Y
    y = lax.rem(me, ROWS_Y)
    side = z * ROWS_Y + (1 - y)

    def hid_at(zz, yy):
        return zz * ROWS_Y + yy

    def cols(c):
        return pl.ds(starts[c], widths[c])

    tok_in = pltpu.make_async_copy(tok_hbm, tok, in_sem.at[0])
    gain_in = pltpu.make_async_copy(gain_hbm, gain, in_sem.at[1])
    kw_in = pltpu.make_async_copy(kw_hbm, kw, in_sem.at[2])
    qw_in = pltpu.make_async_copy(qw_hbm, qw, in_sem.at[3])
    late_in = [
        pltpu.make_async_copy(qs_hbm, qs, in_sem.at[4]),
        pltpu.make_async_copy(ks_hbm, ks, in_sem.at[5]),
        pltpu.make_async_copy(keys_hbm, keys, in_sem.at[6]),
        pltpu.make_async_copy(vals_hbm, vals, in_sem.at[7]),
        pltpu.make_async_copy(len_hbm, lens, in_sem.at[8]),
    ]
    tok_in.start()

    barrier = pltpu.get_barrier_semaphore()

    @pl.when(z + 1 < z_count)
    def _():
        pl.semaphore_signal(barrier, inc=1, device_id={"hid": hid_at(z + 1, y)}, device_id_type=MESH)

    @pl.when(z > 0)
    def _():
        pl.semaphore_signal(barrier, inc=1, device_id={"hid": hid_at(z - 1, y)}, device_id_type=MESH)

    pl.semaphore_signal(barrier, inc=1, device_id={"hid": side}, device_id_type=MESH)
    pl.semaphore_signal(barrier, inc=1, device_id={"wid": other}, device_id_type=MESH)
    gain_in.start()
    kw_in.start()
    qw_in.start()
    for copy in late_in:
        copy.start()

    tok_in.wait()
    row_sum = jnp.zeros((own_rows, 1), jnp.float32)
    row_squares = jnp.zeros((own_rows, 1), jnp.float32)
    for c in range(len(widths)):
        block = tok[:, cols(c)].astype(jnp.float32)
        row_sum += jnp.sum(block, axis=1, keepdims=True)
        row_squares += jnp.sum(block * block, axis=1, keepdims=True)
    lane = lax.broadcasted_iota(jnp.int32, (own_rows, 128), 1)
    stat_mine[...] = jnp.where(lane < 64, row_sum, row_squares)

    ends = (z == 0).astype(jnp.int32) + (z == z_count - 1).astype(jnp.int32)
    pl.semaphore_wait(barrier, 4 - ends)

    def pair(src, dst, k):
        return pltpu.make_async_remote_copy(
            src_ref=src, dst_ref=dst, send_sem=pair_sem.at[0, k], recv_sem=pair_sem.at[1, k],
            device_id={"wid": other}, device_id_type=MESH,
        )

    stat_pair = pair(stat_mine, stat_other, 0)
    stat_pair.start()
    gain_in.wait()
    stat_pair.wait()
    both = stat_mine[...] + stat_other[...]
    row_mean = both[:, 0:1] / full_width
    variance = both[:, 64:65] / full_width - row_mean * row_mean
    row_scale = lax.rsqrt(variance + EPSILON)

    def normalise(c):
        block = tok[:, cols(c)].astype(jnp.float32)
        gat[me, :, cols(c)] = (
            (block - row_mean) * row_scale * gain[:, cols(c)]
        ).astype(jnp.bfloat16)

    start = lambda copy: copy.start()
    finish = lambda copy: copy.wait_send()

    def target_of(link):
        if link == UP:
            return hid_at(z + 1, y)
        if link == DOWN:
            return hid_at(z - 1, y)
        return side

    def send(zz, c, link):
        place = gat.at[hid_at(zz, y), :, cols(c)]
        if link == SIDE:
            recv = side_sem.at[c]
        else:
            recv = line_sem.at[zz, c]
        return pltpu.make_async_remote_copy(
            src_ref=place, dst_ref=place, send_sem=send_sem.at[link, zz], recv_sem=recv,
            device_id={"hid": target_of(link)}, device_id_type=MESH,
        )

    def send_turned(zz, link):
        place = gat.at[hid_at(zz, 1 - y), :, cols(turned)]
        return pltpu.make_async_remote_copy(
            src_ref=place, dst_ref=place, send_sem=turn_send.at[link, zz], recv_sem=turn_sem.at[zz],
            device_id={"hid": target_of(link)}, device_id_type=MESH,
        )

    def arrived(place, sem):
        pltpu.make_async_remote_copy(
            src_ref=place, dst_ref=place, send_sem=send_sem.at[SIDE, 0], recv_sem=sem,
            device_id={"hid": side}, device_id_type=MESH,
        ).wait_recv()

    def line_arrived(zz, c):
        arrived(gat.at[hid_at(zz, y), :, cols(c)], line_sem.at[zz, c])

    def turned_arrived(zz):
        arrived(gat.at[hid_at(zz, 1 - y), :, cols(turned)], turn_sem.at[zz])

    def side_arrived(c):
        if c == turned:
            arrived(gat.at[side, :, cols(c)], side_sem.at[c])
        else:
            arrived(gat.at[pl.ds(0, z_count), :, cols(c)], side_sem.at[c])

    def onward(link, act):
        if link == UP:
            @pl.when(z + 1 < z_count)
            def _():
                act()
        else:
            @pl.when(z > 0)
            def _():
                act()

    def own_sends(c):
        for link in (UP, DOWN):
            onward(link, lambda: send(z, c, link).start())
        send(z, c, SIDE).start()

    def sources_at(k, visit):
        @pl.when(z - k >= 0)
        def _():
            visit(z - k, UP)

        @pl.when(z + k < z_count)
        def _():
            visit(z + k, DOWN)

    def relay(k, c):
        def visit(zz, link):
            line_arrived(zz, c)
            onward(link, lambda: send(zz, c, link).start())
            if c != turned:
                send(zz, c, SIDE).start()

        sources_at(k, visit)

    def relay_turned(k):
        def visit(zz, link):
            line_arrived(zz, turned)
            onward(link, lambda: send(zz, turned, link).start())
            turned_arrived(zz)
            onward(link, lambda: send_turned(zz, link).start())

        sources_at(k, visit)

    def turn():
        side_arrived(turned)
        for link in (UP, DOWN):
            onward(link, lambda: send_turned(z, link).start())

    own_order = list(range(TURN_OWN)) + [turned] + list(range(TURN_OWN, plain))
    pending = list(own_order)
    normalise(pending[0])
    for i in range(AHEAD):
        normalise(own_order[i + 1])
        own_sends(pending.pop(0))
    for c in own_order[AHEAD + 1 :]:
        normalise(c)

    kv_parts = len(widths)

    def kv_step(c):
        part = jnp.dot(gat[me, :, cols(c)], kw[cols(c), :], preferred_element_type=jnp.float32)
        part = part.reshape(kv_acc.shape)
        if c == 0:
            kv_acc[...] = part
        else:
            kv_acc[...] += part

    kv_pair = pair(kv_acc.at[other], kv_rx, 1)

    def operand(c):
        return gat[:, :, cols(c)].reshape(hid_count * own_rows, widths[c])

    def product(c, n):
        columns = pl.ds(pl.multiple_of(n * head_dim, head_dim), head_dim)
        part = jnp.dot(operand(c), qw[cols(c), columns], preferred_element_type=jnp.float32)
        return part.reshape(acc.shape[1:])

    def compute(c):
        def one(n, carry):
            if c == 0:
                acc[n] = product(c, n)
            else:
                acc[n] += product(c, n)
            return carry

        lax.fori_loop(0, tiles, one, 0)

    rounds = plain + z_count - 2 + max(BEHIND, 0)
    rounds = max(rounds, TURN_AT + 1 + TURN_STEP * (z_count - 1))
    kv_done = 0
    for r in range(rounds):
        if pending:
            own_sends(pending.pop(0))
        for k in range(1, z_count):
            c = r - (k - 1)
            if 0 <= c < plain:
                relay(k, c)
        if r == 0:
            kw_in.wait()
        for _ in range(2):
            if kv_done < kv_parts:
                kv_step(kv_done)
                kv_done += 1
                if kv_done == kv_parts:
                    kv_pair.start()
        if r == TURN_AT:
            turn()
        if r > TURN_AT and (r - TURN_AT) % TURN_STEP == 0:
            k = (r - TURN_AT) // TURN_STEP
            if 1 <= k < z_count:
                relay_turned(k)
        c = r - (z_count - 2) - BEHIND
        if c == 0:
            qw_in.wait()
        if 0 <= c < plain - 1:
            side_arrived(c)
            compute(c)
    kv_pair.wait()
    for copy in late_in:
        copy.wait()
    kv_new[...] = ((kv_acc[core] + kv_rx[...]) * ks[...]).astype(jnp.bfloat16)
    new_out = pltpu.make_async_copy(kv_new, new_ref, out_sem.at[0])
    new_out.start()
    for c in range(max(0, rounds - (z_count - 2) - BEHIND), plain - 1):
        side_arrived(c)
        compute(c)
    compute(turned)

    def acc_copy(n):
        return pltpu.make_async_remote_copy(
            src_ref=acc.at[n, :, other], dst_ref=acc_rx.at[n],
            send_sem=acc_send.at[0], recv_sem=acc_recv.at[n],
            device_id={"wid": other}, device_id_type=MESH,
        )

    def q_copy(n, d):
        target = lax.rem(me + d, hid_count)
        return pltpu.make_async_remote_copy(
            src_ref=q_tx.at[n, target], dst_ref=q_rx.at[n, me],
            send_sem=q_send.at[0], recv_sem=q_recv.at[n],
            device_id={"hid": target}, device_id_type=MESH,
        )

    last = plain - 1
    side_arrived(last)
    for n in range(tiles):
        acc[n] += product(last, n)
        acc_copy(n).start()
    for n in range(tiles):
        acc_copy(n).wait_recv()
        total = acc[n, :, core] + acc_rx[n]
        scale = qs[:, pl.ds(n * head_dim, head_dim)]
        q_tx[n] = (total * scale[None]).astype(jnp.bfloat16)
        for d in range(1, hid_count):
            q_copy(n, d).start()
        q_rx[n, me] = q_tx[n, me]

    def whole(zz, link):
        place = gat.at[hid_at(zz, y)]
        if link == SIDE:
            place = gat.at[hid_at(zz, y), :, pl.ds(0, starts[turned])]
        return pltpu.make_async_remote_copy(
            src_ref=place, dst_ref=place, send_sem=send_sem.at[link, zz], recv_sem=side_sem.at[0],
            device_id={"hid": side}, device_id_type=MESH,
        )

    own_place = gat.at[me]
    for link in (UP, DOWN):
        onward(link, lambda: whole(z, link).wait_send())
        onward(link, lambda: send_turned(z, link).wait_send())
    pltpu.make_async_remote_copy(
        src_ref=own_place, dst_ref=own_place, send_sem=send_sem.at[SIDE, z], recv_sem=side_sem.at[0],
        device_id={"hid": side}, device_id_type=MESH,
    ).wait_send()

    def drain(zz, link):
        onward(link, lambda: whole(zz, link).wait_send())
        onward(link, lambda: send_turned(zz, link).wait_send())
        whole(zz, SIDE).wait_send()

    for k in range(1, z_count):
        sources_at(k, drain)

    for n in range(tiles):
        place = q_rx.at[n, pl.ds(0, hid_count - 1)]
        pltpu.make_async_remote_copy(
            src_ref=place, dst_ref=place, send_sem=q_send.at[0], recv_sem=q_recv.at[n],
            device_id={"hid": side}, device_id_type=MESH,
        ).wait_recv()

    heads = hid_count * tiles
    cache_len = keys.shape[1]
    inv_root = head_dim ** (-0.5)
    for n in range(tiles):
        for h in range(hid_count):
            q_f32[h * tiles + n] = q_rx[n, h].astype(jnp.float32)
    position = lax.broadcasted_iota(jnp.int32, (heads, cache_len), 1)
    entries = kv_new[...].astype(jnp.float32)
    for r in range(req):
        query = q_f32[:, r, :]
        score = lax.dot_general(
            query.astype(jnp.bfloat16), keys[r], (((1,), (1,)), ((), ())),
            preferred_element_type=jnp.float32,
        ) * inv_root
        score = jnp.where(position < lens[r], score, -jnp.inf)
        own = jnp.sum(query * entries[r : r + 1, :head_dim], axis=1, keepdims=True) * inv_root
        peak = jnp.maximum(jnp.max(score, axis=1, keepdims=True), own)
        weight = jnp.exp(score - peak)
        own_weight = jnp.exp(own - peak)
        denom = jnp.sum(weight, axis=1, keepdims=True) + own_weight
        weight = (weight / denom).astype(jnp.bfloat16)
        own_weight = (own_weight / denom).astype(jnp.bfloat16).astype(jnp.float32)
        mixed = jnp.dot(weight, vals[r], preferred_element_type=jnp.float32)
        o_f32[:, r, :] = mixed + own_weight * entries[r : r + 1, head_dim:]
    for h in range(heads):
        att[:, h * head_dim : (h + 1) * head_dim] = o_f32[h].astype(jnp.bfloat16)
    att_out = pltpu.make_async_copy(att, att_ref, out_sem.at[1])
    att_out.start()
    sent = acc.at[:, :, other]
    pltpu.make_async_remote_copy(
        src_ref=sent, dst_ref=acc_rx, send_sem=acc_send.at[0], recv_sem=acc_recv.at[0],
        device_id={"wid": other}, device_id_type=MESH,
    ).wait_send()
    sent = q_tx.at[:, pl.ds(0, hid_count - 1)]
    pltpu.make_async_remote_copy(
        src_ref=sent, dst_ref=sent, send_sem=q_send.at[0], recv_sem=q_recv.at[0],
        device_id={"hid": side}, device_id_type=MESH,
    ).wait_send()
    new_out.wait()
    att_out.wait()


def hand_on(att_ref, new_ref, att_out, new_out):
    att_out[...] = att_ref[...]
    new_out[...] = new_ref[...]


def body(
    tokens, norm_gain, query_weight, query_scale, kv_weight, kv_scale,
    keys_cache, values_cache, lengths,
):
    hid_count = lax.axis_size("hid")
    wid_count = lax.axis_size("wid")
    own_rows, half_width = tokens.shape
    local_cols = query_weight.shape[1]
    req, cache_len, head_dim = keys_cache.shape
    tiles = local_cols // head_dim
    heads = hid_count * tiles
    z_count = hid_count // ROWS_Y
    chunks = len(TWELFTHS)
    kv_cols = kv_weight.shape[1]
    bf16, f32 = jnp.bfloat16, jnp.float32
    dma = pltpu.SemaphoreType.DMA
    vm = pltpu.VMEM
    scratch = [
        vm((own_rows, half_width), bf16),
        vm((1, half_width), f32),
        vm((half_width, local_cols), bf16),
        vm((1, local_cols), f32),
        vm((half_width, kv_cols), bf16),
        vm((1, kv_cols), f32),
        vm(keys_cache.shape, bf16),
        vm(values_cache.shape, bf16),
        pltpu.SMEM(lengths.shape, jnp.int32),
        vm((hid_count, own_rows, half_width), bf16),
        vm((own_rows, 128), f32),
        vm((own_rows, 128), f32),
        vm((tiles, hid_count, wid_count, req, head_dim), f32),
        vm((tiles, hid_count, req, head_dim), f32),
        vm((wid_count, req, kv_cols), f32),
        vm((req, kv_cols), f32),
        vm((req, kv_cols), bf16),
        vm((tiles, hid_count, req, head_dim), bf16),
        vm((tiles, hid_count, req, head_dim), bf16),
        vm((heads, req, head_dim), f32),
        vm((heads, req, head_dim), f32),
        vm((req, heads * head_dim), bf16),
        dma((9,)),
        dma((2, 2)),
        dma((3, z_count)),
        dma((2, z_count)),
        dma((z_count, chunks)),
        dma((chunks,)),
        dma((z_count,)),
        dma((1,)),
        dma((tiles,)),
        dma((1,)),
        dma((tiles,)),
        dma((2,)),
    ]
    hbm = pl.BlockSpec(memory_space=pl.ANY)
    attended, new_entries = pl.pallas_call(
        functools.partial(kernel, hid_count, wid_count),
        out_shape=(
            jax.ShapeDtypeStruct((req, heads * head_dim), bf16),
            jax.ShapeDtypeStruct((req, kv_cols), bf16),
        ),
        in_specs=[hbm] * 9,
        out_specs=(hbm, hbm),
        scratch_shapes=scratch,
        compiler_params=pltpu.CompilerParams(
            collective_id=0, has_side_effects=True, vmem_limit_bytes=60 * 1024 * 1024
        ),
    )(
        tokens, norm_gain.reshape(1, -1), query_weight, query_scale.reshape(1, -1),
        kv_weight, kv_scale.reshape(1, -1), keys_cache, values_cache, lengths,
    )
    whole = pl.BlockSpec(memory_space=pltpu.VMEM)
    return pl.pallas_call(
        hand_on,
        out_shape=(
            jax.ShapeDtypeStruct(attended.shape, bf16),
            jax.ShapeDtypeStruct(new_entries.shape, bf16),
        ),
        in_specs=[whole, whole],
        out_specs=(whole, whole),
    )(attended, new_entries)


def solution(mesh):
    placed = (
        P(("groups", "hid"), "wid"),
        P("wid"),
        P("wid", "hid"),
        P("hid"),
        P("wid", None),
        P(),
        P(("groups", "hid", "wid"), None, None),
        P(("groups", "hid", "wid"), None, None),
        P(("groups", "hid", "wid")),
    )
    return jax.shard_map(
        body,
        mesh=mesh,
        in_specs=placed,
        out_specs=(P(("groups", "hid", "wid"), None), P(("groups", "hid", "wid"), None)),
        check_vma=False,
    )
```

```python
import functools

import jax
import jax.numpy as jnp
from jax import lax
from jax.experimental import pallas as pl
from jax.experimental.pallas import tpu as pltpu
from jax.sharding import PartitionSpec as P

EPSILON = 1e-05
ROWS_Y = 2
TWELFTHS = (2, 2, 2, 2, 1, 1, 2)
AHEAD = 2
BEHIND = 2
TURN_OWN = 2
TURN_AT = 3
TURN_STEP = 2
UP, DOWN, SIDE = 0, 1, 2
MESH = pl.DeviceIdType.MESH


def kernel(
    hid_count, wid_count,
    tok_hbm, gain_hbm, qw_hbm, qs_hbm, kw_hbm, ks_hbm, keys_hbm, vals_hbm, len_hbm,
    att_ref, new_ref,
    tok, gain, qw, qs, kw, ks, keys, vals, lens,
    gat, stat_mine, stat_other, acc, acc_rx, kv_acc, kv_rx, kv_new,
    q_tx, q_rx, q_f32, o_f32, scores, weights, att,
    in_sem, pair_sem, send_sem, turn_send, line_sem, side_sem, turn_sem,
    acc_send, acc_recv, q_send, q_recv, out_sem,
):
    own_rows, half_width = tok_hbm.shape
    full_width = half_width * wid_count
    unit = half_width // sum(TWELFTHS)
    widths = [t * unit for t in TWELFTHS]
    starts = [sum(widths[:c]) for c in range(len(widths))]
    plain = len(widths) - 1
    turned = plain
    tiles, _, _, req, head_dim = acc.shape
    z_count = hid_count // ROWS_Y
    me = lax.axis_index("hid")
    core = lax.axis_index("wid")
    other = 1 - core
    z = me // ROWS_Y
    y = lax.rem(me, ROWS_Y)
    side = z * ROWS_Y + (1 - y)

    def hid_at(zz, yy):
        return zz * ROWS_Y + yy

    def cols(c):
        return pl.ds(starts[c], widths[c])

    tok_in = pltpu.make_async_copy(tok_hbm, tok, in_sem.at[0])
    gain_in = pltpu.make_async_copy(gain_hbm, gain, in_sem.at[1])
    kw_in = pltpu.make_async_copy(kw_hbm, kw, in_sem.at[2])
    qw_in = pltpu.make_async_copy(qw_hbm, qw, in_sem.at[3])
    late_in = [
        pltpu.make_async_copy(qs_hbm, qs, in_sem.at[4]),
        pltpu.make_async_copy(ks_hbm, ks, in_sem.at[5]),
        pltpu.make_async_copy(keys_hbm, keys, in_sem.at[6]),
        pltpu.make_async_copy(vals_hbm, vals, in_sem.at[7]),
        pltpu.make_async_copy(len_hbm, lens, in_sem.at[8]),
    ]
    tok_in.start()

    barrier = pltpu.get_barrier_semaphore()

    @pl.when(z + 1 < z_count)
    def _():
        pl.semaphore_signal(barrier, inc=1, device_id={"hid": hid_at(z + 1, y)}, device_id_type=MESH)

    @pl.when(z > 0)
    def _():
        pl.semaphore_signal(barrier, inc=1, device_id={"hid": hid_at(z - 1, y)}, device_id_type=MESH)

    pl.semaphore_signal(barrier, inc=1, device_id={"hid": side}, device_id_type=MESH)
    pl.semaphore_signal(barrier, inc=1, device_id={"wid": other}, device_id_type=MESH)
    gain_in.start()
    kw_in.start()
    qw_in.start()
    for copy in late_in:
        copy.start()

    tok_in.wait()
    row_sum = jnp.zeros((own_rows, 1), jnp.float32)
    row_squares = jnp.zeros((own_rows, 1), jnp.float32)
    for c in range(len(widths)):
        block = tok[:, cols(c)].astype(jnp.float32)
        row_sum += jnp.sum(block, axis=1, keepdims=True)
        row_squares += jnp.sum(block * block, axis=1, keepdims=True)
    lane = lax.broadcasted_iota(jnp.int32, (own_rows, 128), 1)
    stat_mine[...] = jnp.where(lane < 64, row_sum, row_squares)

    ends = (z == 0).astype(jnp.int32) + (z == z_count - 1).astype(jnp.int32)
    pl.semaphore_wait(barrier, 4 - ends)

    def pair(src, dst, k):
        return pltpu.make_async_remote_copy(
            src_ref=src, dst_ref=dst, send_sem=pair_sem.at[0, k], recv_sem=pair_sem.at[1, k],
            device_id={"wid": other}, device_id_type=MESH,
        )

    stat_pair = pair(stat_mine, stat_other, 0)
    stat_pair.start()
    gain_in.wait()
    stat_pair.wait()
    both = stat_mine[...] + stat_other[...]
    row_mean = both[:, 0:1] / full_width
    variance = both[:, 64:65] / full_width - row_mean * row_mean
    row_scale = lax.rsqrt(variance + EPSILON)

    def normalise(c):
        block = tok[:, cols(c)].astype(jnp.float32)
        gat[me, :, cols(c)] = (
            (block - row_mean) * row_scale * gain[:, cols(c)]
        ).astype(jnp.bfloat16)

    start = lambda copy: copy.start()
    finish = lambda copy: copy.wait_send()

    def target_of(link):
        if link == UP:
            return hid_at(z + 1, y)
        if link == DOWN:
            return hid_at(z - 1, y)
        return side

    def send(zz, c, link):
        place = gat.at[hid_at(zz, y), :, cols(c)]
        if link == SIDE:
            recv = side_sem.at[c]
        else:
            recv = line_sem.at[zz, c]
        return pltpu.make_async_remote_copy(
            src_ref=place, dst_ref=place, send_sem=send_sem.at[link, zz], recv_sem=recv,
            device_id={"hid": target_of(link)}, device_id_type=MESH,
        )

    def send_turned(zz, link):
        place = gat.at[hid_at(zz, 1 - y), :, cols(turned)]
        return pltpu.make_async_remote_copy(
            src_ref=place, dst_ref=place, send_sem=turn_send.at[link, zz], recv_sem=turn_sem.at[zz],
            device_id={"hid": target_of(link)}, device_id_type=MESH,
        )

    def arrived(place, sem):
        pltpu.make_async_remote_copy(
            src_ref=place, dst_ref=place, send_sem=send_sem.at[SIDE, 0], recv_sem=sem,
            device_id={"hid": side}, device_id_type=MESH,
        ).wait_recv()

    def line_arrived(zz, c):
        arrived(gat.at[hid_at(zz, y), :, cols(c)], line_sem.at[zz, c])

    def turned_arrived(zz):
        arrived(gat.at[hid_at(zz, 1 - y), :, cols(turned)], turn_sem.at[zz])

    def side_arrived(c):
        if c == turned:
            arrived(gat.at[side, :, cols(c)], side_sem.at[c])
        else:
            arrived(gat.at[pl.ds(0, z_count), :, cols(c)], side_sem.at[c])

    def onward(link, act):
        if link == UP:
            @pl.when(z + 1 < z_count)
            def _():
                act()
        else:
            @pl.when(z > 0)
            def _():
                act()

    def own_sends(c):
        for link in (UP, DOWN):
            onward(link, lambda: send(z, c, link).start())
        send(z, c, SIDE).start()

    def sources_at(k, visit):
        @pl.when(z - k >= 0)
        def _():
            visit(z - k, UP)

        @pl.when(z + k < z_count)
        def _():
            visit(z + k, DOWN)

    def relay(k, c):
        def visit(zz, link):
            line_arrived(zz, c)
            onward(link, lambda: send(zz, c, link).start())
            if c != turned:
                send(zz, c, SIDE).start()

        sources_at(k, visit)

    def relay_turned(k):
        def visit(zz, link):
            line_arrived(zz, turned)
            onward(link, lambda: send(zz, turned, link).start())
            turned_arrived(zz)
            onward(link, lambda: send_turned(zz, link).start())

        sources_at(k, visit)

    def turn():
        side_arrived(turned)
        for link in (UP, DOWN):
            onward(link, lambda: send_turned(z, link).start())

    own_order = list(range(TURN_OWN)) + [turned] + list(range(TURN_OWN, plain))
    pending = list(own_order)
    normalise(pending[0])
    for i in range(AHEAD):
        normalise(own_order[i + 1])
        own_sends(pending.pop(0))
    for c in own_order[AHEAD + 1 :]:
        normalise(c)

    kv_parts = len(widths)

    def kv_step(c):
        part = jnp.dot(gat[me, :, cols(c)], kw[cols(c), :], preferred_element_type=jnp.float32)
        part = part.reshape(kv_acc.shape)
        if c == 0:
            kv_acc[...] = part
        else:
            kv_acc[...] += part

    kv_pair = pair(kv_acc.at[other], kv_rx, 1)

    def operand(c):
        return gat[:, :, cols(c)].reshape(hid_count * own_rows, widths[c])

    def product(c, n):
        columns = pl.ds(pl.multiple_of(n * head_dim, head_dim), head_dim)
        part = jnp.dot(operand(c), qw[cols(c), columns], preferred_element_type=jnp.float32)
        return part.reshape(acc.shape[1:])

    def compute(c):
        def one(n, carry):
            if c == 0:
                acc[n] = product(c, n)
            else:
                acc[n] += product(c, n)
            return carry

        lax.fori_loop(0, tiles, one, 0)

    rounds = plain + z_count - 2 + max(BEHIND, 0)
    rounds = max(rounds, TURN_AT + 1 + TURN_STEP * (z_count - 1))
    kv_done = 0
    for r in range(rounds):
        if pending:
            own_sends(pending.pop(0))
        for k in range(1, z_count):
            c = r - (k - 1)
            if 0 <= c < plain:
                relay(k, c)
        if r == 0:
            kw_in.wait()
        for _ in range(2):
            if kv_done < kv_parts:
                kv_step(kv_done)
                kv_done += 1
                if kv_done == kv_parts:
                    kv_pair.start()
        if r == TURN_AT:
            turn()
        if r > TURN_AT and (r - TURN_AT) % TURN_STEP == 0:
            k = (r - TURN_AT) // TURN_STEP
            if 1 <= k < z_count:
                relay_turned(k)
        c = r - (z_count - 2) - BEHIND
        if c == 0:
            qw_in.wait()
        if 0 <= c < plain - 1:
            side_arrived(c)
            compute(c)
    kv_pair.wait()
    for copy in late_in:
        copy.wait()
    kv_new[...] = ((kv_acc[core] + kv_rx[...]) * ks[...]).astype(jnp.bfloat16)
    new_out = pltpu.make_async_copy(kv_new, new_ref, out_sem.at[0])
    new_out.start()
    for c in range(max(0, rounds - (z_count - 2) - BEHIND), plain - 1):
        side_arrived(c)
        compute(c)
    compute(turned)

    def acc_copy(n):
        return pltpu.make_async_remote_copy(
            src_ref=acc.at[n, :, other], dst_ref=acc_rx.at[n],
            send_sem=acc_send.at[0], recv_sem=acc_recv.at[n],
            device_id={"wid": other}, device_id_type=MESH,
        )

    def q_copy(n, d):
        target = lax.rem(me + d, hid_count)
        return pltpu.make_async_remote_copy(
            src_ref=q_tx.at[n, target], dst_ref=q_rx.at[n, me],
            send_sem=q_send.at[0], recv_sem=q_recv.at[n],
            device_id={"hid": target}, device_id_type=MESH,
        )

    last = plain - 1
    side_arrived(last)
    for n in range(tiles):
        acc[n] += product(last, n)
        acc_copy(n).start()
    for n in range(tiles):
        acc_copy(n).wait_recv()
        total = acc[n, :, core] + acc_rx[n]
        scale = qs[:, pl.ds(n * head_dim, head_dim)]
        q_tx[n] = (total * scale[None]).astype(jnp.bfloat16)
        for d in range(1, hid_count):
            q_copy(n, d).start()
        q_rx[n, me] = q_tx[n, me]

    def whole(zz, link):
        place = gat.at[hid_at(zz, y)]
        if link == SIDE:
            place = gat.at[hid_at(zz, y), :, pl.ds(0, starts[turned])]
        return pltpu.make_async_remote_copy(
            src_ref=place, dst_ref=place, send_sem=send_sem.at[link, zz], recv_sem=side_sem.at[0],
            device_id={"hid": side}, device_id_type=MESH,
        )

    own_place = gat.at[me]
    for link in (UP, DOWN):
        onward(link, lambda: whole(z, link).wait_send())
        onward(link, lambda: send_turned(z, link).wait_send())
    pltpu.make_async_remote_copy(
        src_ref=own_place, dst_ref=own_place, send_sem=send_sem.at[SIDE, z], recv_sem=side_sem.at[0],
        device_id={"hid": side}, device_id_type=MESH,
    ).wait_send()

    def drain(zz, link):
        onward(link, lambda: whole(zz, link).wait_send())
        onward(link, lambda: send_turned(zz, link).wait_send())
        whole(zz, SIDE).wait_send()

    for k in range(1, z_count):
        sources_at(k, drain)

    for n in range(tiles):
        place = q_rx.at[n, pl.ds(0, hid_count - 1)]
        pltpu.make_async_remote_copy(
            src_ref=place, dst_ref=place, send_sem=q_send.at[0], recv_sem=q_recv.at[n],
            device_id={"hid": side}, device_id_type=MESH,
        ).wait_recv()

    heads = hid_count * tiles
    cache_len = keys.shape[1]
    inv_root = head_dim ** (-0.5)
    for n in range(tiles):
        for h in range(hid_count):
            q_f32[h * tiles + n] = q_rx[n, h].astype(jnp.float32)
    position = lax.broadcasted_iota(jnp.int32, (heads, cache_len), 1)
    entries = kv_new[...].astype(jnp.float32)
    def query_of(r):
        return q_f32[:, r, :]

    def score(r):
        scores[r] = lax.dot_general(
            query_of(r).astype(jnp.bfloat16), keys[r], (((1,), (1,)), ((), ())),
            preferred_element_type=jnp.float32,
        )

    def weigh(r):
        live = jnp.where(position < lens[r], scores[r] * inv_root, -jnp.inf)
        own = jnp.sum(query_of(r) * entries[r : r + 1, :head_dim], axis=1, keepdims=True) * inv_root
        peak = jnp.maximum(jnp.max(live, axis=1, keepdims=True), own)
        weight = jnp.exp(live - peak)
        own_weight = jnp.exp(own - peak)
        inverse = 1.0 / (jnp.sum(weight, axis=1, keepdims=True) + own_weight)
        weights[r] = (weight * inverse).astype(jnp.bfloat16)
        return (own_weight * inverse).astype(jnp.bfloat16).astype(jnp.float32)

    def mix(r, own_weight):
        mixed = jnp.dot(weights[r], vals[r], preferred_element_type=jnp.float32)
        o_f32[:, r, :] = mixed + own_weight * entries[r : r + 1, head_dim:]

    own_weights = []
    for r in range(min(2, req)):
        score(r)
    for r in range(req):
        own_weights.append(weigh(r))
        if r + 2 < req:
            score(r + 2)
        if r >= 1:
            mix(r - 1, own_weights[r - 1])
    mix(req - 1, own_weights[req - 1])
    for h in range(heads):
        att[:, h * head_dim : (h + 1) * head_dim] = o_f32[h].astype(jnp.bfloat16)
    att_out = pltpu.make_async_copy(att, att_ref, out_sem.at[1])
    att_out.start()
    sent = acc.at[:, :, other]
    pltpu.make_async_remote_copy(
        src_ref=sent, dst_ref=acc_rx, send_sem=acc_send.at[0], recv_sem=acc_recv.at[0],
        device_id={"wid": other}, device_id_type=MESH,
    ).wait_send()
    sent = q_tx.at[:, pl.ds(0, hid_count - 1)]
    pltpu.make_async_remote_copy(
        src_ref=sent, dst_ref=sent, send_sem=q_send.at[0], recv_sem=q_recv.at[0],
        device_id={"hid": side}, device_id_type=MESH,
    ).wait_send()
    new_out.wait()
    att_out.wait()


def hand_on(att_ref, new_ref, att_out, new_out):
    att_out[...] = att_ref[...]
    new_out[...] = new_ref[...]


def body(
    tokens, norm_gain, query_weight, query_scale, kv_weight, kv_scale,
    keys_cache, values_cache, lengths,
):
    hid_count = lax.axis_size("hid")
    wid_count = lax.axis_size("wid")
    own_rows, half_width = tokens.shape
    local_cols = query_weight.shape[1]
    req, cache_len, head_dim = keys_cache.shape
    tiles = local_cols // head_dim
    heads = hid_count * tiles
    z_count = hid_count // ROWS_Y
    chunks = len(TWELFTHS)
    kv_cols = kv_weight.shape[1]
    bf16, f32 = jnp.bfloat16, jnp.float32
    dma = pltpu.SemaphoreType.DMA
    vm = pltpu.VMEM
    scratch = [
        vm((own_rows, half_width), bf16),
        vm((1, half_width), f32),
        vm((half_width, local_cols), bf16),
        vm((1, local_cols), f32),
        vm((half_width, kv_cols), bf16),
        vm((1, kv_cols), f32),
        vm(keys_cache.shape, bf16),
        vm(values_cache.shape, bf16),
        pltpu.SMEM(lengths.shape, jnp.int32),
        vm((hid_count, own_rows, half_width), bf16),
        vm((own_rows, 128), f32),
        vm((own_rows, 128), f32),
        vm((tiles, hid_count, wid_count, req, head_dim), f32),
        vm((tiles, hid_count, req, head_dim), f32),
        vm((wid_count, req, kv_cols), f32),
        vm((req, kv_cols), f32),
        vm((req, kv_cols), bf16),
        vm((tiles, hid_count, req, head_dim), bf16),
        vm((tiles, hid_count, req, head_dim), bf16),
        vm((heads, req, head_dim), f32),
        vm((heads, req, head_dim), f32),
        vm((req, heads, cache_len), f32),
        vm((req, heads, cache_len), bf16),
        vm((req, heads * head_dim), bf16),
        dma((9,)),
        dma((2, 2)),
        dma((3, z_count)),
        dma((2, z_count)),
        dma((z_count, chunks)),
        dma((chunks,)),
        dma((z_count,)),
        dma((1,)),
        dma((tiles,)),
        dma((1,)),
        dma((tiles,)),
        dma((2,)),
    ]
    hbm = pl.BlockSpec(memory_space=pl.ANY)
    attended, new_entries = pl.pallas_call(
        functools.partial(kernel, hid_count, wid_count),
        out_shape=(
            jax.ShapeDtypeStruct((req, heads * head_dim), bf16),
            jax.ShapeDtypeStruct((req, kv_cols), bf16),
        ),
        in_specs=[hbm] * 9,
        out_specs=(hbm, hbm),
        scratch_shapes=scratch,
        compiler_params=pltpu.CompilerParams(
            collective_id=0, has_side_effects=True, vmem_limit_bytes=60 * 1024 * 1024
        ),
    )(
        tokens, norm_gain.reshape(1, -1), query_weight, query_scale.reshape(1, -1),
        kv_weight, kv_scale.reshape(1, -1), keys_cache, values_cache, lengths,
    )
    whole = pl.BlockSpec(memory_space=pltpu.VMEM)
    return pl.pallas_call(
        hand_on,
        out_shape=(
            jax.ShapeDtypeStruct(attended.shape, bf16),
            jax.ShapeDtypeStruct(new_entries.shape, bf16),
        ),
        in_specs=[whole, whole],
        out_specs=(whole, whole),
    )(attended, new_entries)


def solution(mesh):
    placed = (
        P(("groups", "hid"), "wid"),
        P("wid"),
        P("wid", "hid"),
        P("hid"),
        P("wid", None),
        P(),
        P(("groups", "hid", "wid"), None, None),
        P(("groups", "hid", "wid"), None, None),
        P(("groups", "hid", "wid")),
    )
    return jax.shard_map(
        body,
        mesh=mesh,
        in_specs=placed,
        out_specs=(P(("groups", "hid", "wid"), None), P(("groups", "hid", "wid"), None)),
        check_vma=False,
    )
```

```python
import functools

import jax
import jax.numpy as jnp
from jax import lax
from jax.experimental import pallas as pl
from jax.experimental.pallas import tpu as pltpu
from jax.sharding import PartitionSpec as P

EPSILON = 1e-05
ROWS_Y = 2
TWELFTHS = (3, 1, 2, 2, 1, 1, 2)
LANES = 128
BLOCK = 4
AHEAD = 2
BEHIND = 2
TURN_OWN = 2
TURN_AT = 3
TURN_STEP = 2
UP, DOWN, SIDE = 0, 1, 2
MESH = pl.DeviceIdType.MESH


def kernel(
    hid_count, wid_count,
    tok_hbm, gain_hbm, qw_hbm, qs_hbm, kw_hbm, ks_hbm, keys_hbm, vals_hbm, len_hbm,
    att_ref, new_ref,
    tok, gain, qw, qs, kw, ks, keys, vals, lens,
    gat, stat_mine, stat_other, acc, acc_rx, kv_acc, kv_rx, kv_new,
    q_tx, q_rx, q_f32, o_f32, scores, weights, att, first,
    in_sem, pair_sem, send_sem, turn_send, line_sem, side_sem, turn_sem,
    acc_send, acc_recv, q_send, q_recv, out_sem,
):
    own_rows, half_width = tok_hbm.shape
    full_width = half_width * wid_count
    unit = half_width // sum(TWELFTHS)
    widths = [t * unit for t in TWELFTHS]
    starts = [sum(widths[:c]) for c in range(len(widths))]
    plain = len(widths) - 1
    turned = plain
    tiles, _, _, req, head_dim = acc.shape
    z_count = hid_count // ROWS_Y
    me = lax.axis_index("hid")
    core = lax.axis_index("wid")
    other = 1 - core
    z = me // ROWS_Y
    y = lax.rem(me, ROWS_Y)
    side = z * ROWS_Y + (1 - y)

    def hid_at(zz, yy):
        return zz * ROWS_Y + yy

    def cols(c):
        return pl.ds(starts[c], widths[c])

    def held(c):
        return pl.ds(starts[c] + (LANES if c > 1 else 0), widths[c])

    def sent(c):
        return pl.ds(held(c).start, widths[c] + (LANES if c == 1 else 0))

    beside = pl.ds(starts[2], LANES)

    tok_in = pltpu.make_async_copy(tok_hbm, tok, in_sem.at[0])
    gain_in = pltpu.make_async_copy(gain_hbm, gain, in_sem.at[1])
    kw_in = pltpu.make_async_copy(kw_hbm, kw, in_sem.at[2])
    qw_in = pltpu.make_async_copy(qw_hbm, qw, in_sem.at[3])
    late_in = [
        pltpu.make_async_copy(qs_hbm, qs, in_sem.at[4]),
        pltpu.make_async_copy(ks_hbm, ks, in_sem.at[5]),
        pltpu.make_async_copy(keys_hbm, keys, in_sem.at[6]),
        pltpu.make_async_copy(vals_hbm, vals, in_sem.at[7]),
        pltpu.make_async_copy(len_hbm, lens, in_sem.at[8]),
    ]
    tok_in.start()

    barrier = pltpu.get_barrier_semaphore()

    @pl.when(z + 1 < z_count)
    def _():
        pl.semaphore_signal(barrier, inc=1, device_id={"hid": hid_at(z + 1, y)}, device_id_type=MESH)

    @pl.when(z > 0)
    def _():
        pl.semaphore_signal(barrier, inc=1, device_id={"hid": hid_at(z - 1, y)}, device_id_type=MESH)

    pl.semaphore_signal(barrier, inc=1, device_id={"hid": side}, device_id_type=MESH)
    pl.semaphore_signal(barrier, inc=1, device_id={"wid": other}, device_id_type=MESH)
    gain_in.start()
    kw_in.start()
    qw_in.start()
    for copy in late_in:
        copy.start()

    tok_in.wait()
    row_sum = jnp.zeros((own_rows, 1), jnp.float32)
    row_squares = jnp.zeros((own_rows, 1), jnp.float32)
    for c in range(len(widths)):
        block = tok[:, cols(c)].astype(jnp.float32)
        row_sum += jnp.sum(block, axis=1, keepdims=True)
        row_squares += jnp.sum(block * block, axis=1, keepdims=True)
    lane = lax.broadcasted_iota(jnp.int32, (own_rows, 128), 1)
    stat_mine[...] = jnp.where(lane < 64, row_sum, row_squares)

    ends = (z == 0).astype(jnp.int32) + (z == z_count - 1).astype(jnp.int32)
    pl.semaphore_wait(barrier, 4 - ends)

    def pair(src, dst, k):
        return pltpu.make_async_remote_copy(
            src_ref=src, dst_ref=dst, send_sem=pair_sem.at[0, k], recv_sem=pair_sem.at[1, k],
            device_id={"wid": other}, device_id_type=MESH,
        )

    def target_of(link):
        if link == UP:
            return hid_at(z + 1, y)
        if link == DOWN:
            return hid_at(z - 1, y)
        return side

    def send(zz, c, link, own=False):
        place = gat.at[hid_at(zz, y), :, sent(c)]
        source = tok.at[:, cols(0)] if own and c == 0 else place
        if link == SIDE:
            recv = side_sem.at[c]
        else:
            recv = line_sem.at[zz, c]
        return pltpu.make_async_remote_copy(
            src_ref=source, dst_ref=place, send_sem=send_sem.at[link, zz], recv_sem=recv,
            device_id={"hid": target_of(link)}, device_id_type=MESH,
        )

    def send_turned(zz, link):
        place = gat.at[hid_at(zz, 1 - y), :, sent(turned)]
        return pltpu.make_async_remote_copy(
            src_ref=place, dst_ref=place, send_sem=turn_send.at[link, zz], recv_sem=turn_sem.at[zz],
            device_id={"hid": target_of(link)}, device_id_type=MESH,
        )

    def arrived(place, sem):
        pltpu.make_async_remote_copy(
            src_ref=place, dst_ref=place, send_sem=send_sem.at[SIDE, 0], recv_sem=sem,
            device_id={"hid": side}, device_id_type=MESH,
        ).wait_recv()

    def line_arrived(zz, c):
        arrived(gat.at[hid_at(zz, y), :, sent(c)], line_sem.at[zz, c])

    def turned_arrived(zz):
        arrived(gat.at[hid_at(zz, 1 - y), :, sent(turned)], turn_sem.at[zz])

    def side_arrived(c):
        if c == turned:
            arrived(gat.at[side, :, sent(c)], side_sem.at[c])
        else:
            arrived(gat.at[pl.ds(0, z_count), :, sent(c)], side_sem.at[c])

    def onward(link, act):
        if link == UP:
            @pl.when(z + 1 < z_count)
            def _():
                act()
        else:
            @pl.when(z > 0)
            def _():
                act()

    def own_sends(c):
        for link in (UP, DOWN):
            onward(link, lambda: send(z, c, link, True).start())
        send(z, c, SIDE, True).start()

    def sources_at(k, visit):
        @pl.when(z - k >= 0)
        def _():
            visit(z - k, UP)

        @pl.when(z + k < z_count)
        def _():
            visit(z + k, DOWN)

    def relay(k, c):
        def visit(zz, link):
            line_arrived(zz, c)
            onward(link, lambda: send(zz, c, link).start())
            if c != turned:
                send(zz, c, SIDE).start()

        sources_at(k, visit)

    def relay_turned(k):
        def visit(zz, link):
            line_arrived(zz, turned)
            onward(link, lambda: send(zz, turned, link).start())
            turned_arrived(zz)
            onward(link, lambda: send_turned(zz, link).start())

        sources_at(k, visit)

    def turn():
        side_arrived(turned)
        for link in (UP, DOWN):
            onward(link, lambda: send_turned(z, link).start())

    own_order = list(range(TURN_OWN)) + [turned] + list(range(TURN_OWN, plain))
    pending = list(own_order)
    own_sends(pending.pop(0))
    stat_pair = pair(stat_mine, stat_other, 0)
    stat_pair.start()
    gain_in.wait()
    stat_pair.wait()
    both = stat_mine[...] + stat_other[...]
    row_mean = both[:, 0:1] / full_width
    variance = both[:, 64:65] / full_width - row_mean * row_mean
    row_scale = lax.rsqrt(variance + EPSILON)

    def normalise(c):
        block = tok[:, cols(c)].astype(jnp.float32)
        value = ((block - row_mean) * row_scale * gain[:, cols(c)]).astype(jnp.bfloat16)
        if c == 0:
            first[me] = value
        else:
            gat[me, :, held(c)] = value

    def addends(value):
        high = value.astype(jnp.bfloat16).astype(jnp.float32)
        middle = (value - high).astype(jnp.bfloat16).astype(jnp.float32)
        return high, middle, value - high - middle

    def tell():
        told = jnp.zeros((own_rows, LANES), jnp.float32)
        for i, value in enumerate(addends(row_mean) + addends(row_scale)):
            told = jnp.where(lane == i, value, told)
        gat[me, :, beside] = told.astype(jnp.bfloat16)

    def normalise_first():
        def one(h, carry):
            @pl.when(h != me)
            def _():
                told = gat[h, :, beside].astype(jnp.float32)
                mean = told[:, 0:1] + told[:, 1:2] + told[:, 2:3]
                scale = told[:, 3:4] + told[:, 4:5] + told[:, 5:6]
                block = gat[h, :, held(0)].astype(jnp.float32)
                first[h] = ((block - mean) * scale * gain[:, cols(0)]).astype(jnp.bfloat16)

            return carry

        lax.fori_loop(0, hid_count, one, 0)

    normalise(1)
    tell()
    for i in range(1, AHEAD):
        normalise(own_order[i + 1])
        own_sends(pending.pop(0))
    for c in own_order[AHEAD + 1 :] + [0]:
        normalise(c)

    kv_parts = len(widths)

    def kv_step(c):
        rows = first[me] if c == 0 else gat[me, :, held(c)]
        part = jnp.dot(rows, kw[cols(c), :], preferred_element_type=jnp.float32)
        part = part.reshape(kv_acc.shape)
        if c == 0:
            kv_acc[...] = part
        else:
            kv_acc[...] += part

    kv_pair = pair(kv_acc.at[other], kv_rx, 1)

    def operand(c):
        rows = first[...] if c == 0 else gat[:, :, held(c)]
        return rows.reshape(hid_count * own_rows, widths[c])

    def add_product(c, low, high, fresh=False):
        columns = pl.ds(low * head_dim, (high - low) * head_dim)
        part = jnp.dot(operand(c), qw[cols(c), columns], preferred_element_type=jnp.float32)
        for n in range(low, high):
            own = part[:, (n - low) * head_dim : (n - low + 1) * head_dim].reshape(acc.shape[1:])
            acc[n] = own if fresh else acc[n] + own

    def compute(c, fresh=False):
        for low in range(0, tiles, BLOCK):
            add_product(c, low, min(low + BLOCK, tiles), fresh)

    rounds = plain + z_count - 2 + max(BEHIND, 0)
    rounds = max(rounds, TURN_AT + 1 + TURN_STEP * (z_count - 1))
    kv_done = 0
    for r in range(rounds):
        if pending:
            own_sends(pending.pop(0))
        for k in range(1, z_count):
            c = r - (k - 1)
            if 0 <= c < plain:
                relay(k, c)
        if r == 0:
            kw_in.wait()
        for _ in range(2):
            if kv_done < kv_parts:
                kv_step(kv_done)
                kv_done += 1
                if kv_done == kv_parts:
                    kv_pair.start()
        if r == TURN_AT:
            turn()
        if r > TURN_AT and (r - TURN_AT) % TURN_STEP == 0:
            k = (r - TURN_AT) // TURN_STEP
            if 1 <= k < z_count:
                relay_turned(k)
        c = r - (z_count - 2) - BEHIND
        if c == 1:
            qw_in.wait()
            side_arrived(0)
            side_arrived(1)
            normalise_first()
            compute(1, True)
            compute(0)
        elif 1 < c < plain - 1:
            side_arrived(c)
            compute(c)
    kv_pair.wait()
    for copy in late_in:
        copy.wait()
    kv_new[...] = ((kv_acc[core] + kv_rx[...]) * ks[...]).astype(jnp.bfloat16)
    new_out = pltpu.make_async_copy(kv_new, new_ref, out_sem.at[0])
    new_out.start()
    for c in range(max(0, rounds - (z_count - 2) - BEHIND), plain - 1):
        side_arrived(c)
        compute(c)
    compute(turned)

    def acc_copy(n):
        return pltpu.make_async_remote_copy(
            src_ref=acc.at[n, :, other], dst_ref=acc_rx.at[n],
            send_sem=acc_send.at[0], recv_sem=acc_recv.at[n],
            device_id={"wid": other}, device_id_type=MESH,
        )

    def q_copy(n, target):
        return pltpu.make_async_remote_copy(
            src_ref=q_tx.at[n, target], dst_ref=q_rx.at[n, me],
            send_sem=q_send.at[0], recv_sem=q_recv.at[n],
            device_id={"hid": target}, device_id_type=MESH,
        )

    last = plain - 1
    side_arrived(last)
    half = -(-tiles // 2)
    for low in range(0, tiles, half):
        high = min(low + half, tiles)
        add_product(last, low, high)
        for n in range(low, high):
            acc_copy(n).start()
    for n in range(tiles):
        acc_copy(n).wait_recv()
        total = acc[n, :, core] + acc_rx[n]
        scale = qs[:, pl.ds(n * head_dim, head_dim)]
        q_tx[n] = (total * scale[None]).astype(jnp.bfloat16)
        for k in range(z_count - 1, 0, -1):
            def hand_out(zz, link, n=n):
                for yy in (1 - y, y):
                    q_copy(n, hid_at(zz, yy)).start()

            sources_at(k, hand_out)
        q_copy(n, side).start()
        q_rx[n, me] = q_tx[n, me]

    def whole(zz, link):
        place = gat.at[hid_at(zz, y)]
        if link == SIDE:
            place = gat.at[hid_at(zz, y), :, pl.ds(0, sent(turned).start)]
        return pltpu.make_async_remote_copy(
            src_ref=place, dst_ref=place, send_sem=send_sem.at[link, zz], recv_sem=side_sem.at[0],
            device_id={"hid": side}, device_id_type=MESH,
        )

    own_place = gat.at[me]
    for link in (UP, DOWN):
        onward(link, lambda: whole(z, link).wait_send())
        onward(link, lambda: send_turned(z, link).wait_send())
    pltpu.make_async_remote_copy(
        src_ref=own_place, dst_ref=own_place, send_sem=send_sem.at[SIDE, z], recv_sem=side_sem.at[0],
        device_id={"hid": side}, device_id_type=MESH,
    ).wait_send()

    def drain(zz, link):
        onward(link, lambda: whole(zz, link).wait_send())
        onward(link, lambda: send_turned(zz, link).wait_send())
        whole(zz, SIDE).wait_send()

    for k in range(1, z_count):
        sources_at(k, drain)

    for n in range(tiles):
        place = q_rx.at[n, pl.ds(0, hid_count - 1)]
        pltpu.make_async_remote_copy(
            src_ref=place, dst_ref=place, send_sem=q_send.at[0], recv_sem=q_recv.at[n],
            device_id={"hid": side}, device_id_type=MESH,
        ).wait_recv()

    heads = hid_count * tiles
    cache_len = keys.shape[1]
    inv_root = head_dim ** (-0.5)
    for n in range(tiles):
        for h in range(hid_count):
            q_f32[h * tiles + n] = q_rx[n, h].astype(jnp.float32)
    position = lax.broadcasted_iota(jnp.int32, (heads, cache_len), 1)
    entries = kv_new[...].astype(jnp.float32)
    def query_of(r):
        return q_f32[:, r, :]

    def score(r):
        scores[r] = lax.dot_general(
            query_of(r).astype(jnp.bfloat16), keys[r], (((1,), (1,)), ((), ())),
            preferred_element_type=jnp.float32,
        )

    def weigh(r):
        live = jnp.where(position < lens[r], scores[r] * inv_root, -jnp.inf)
        own = jnp.sum(query_of(r) * entries[r : r + 1, :head_dim], axis=1, keepdims=True) * inv_root
        peak = jnp.maximum(jnp.max(live, axis=1, keepdims=True), own)
        weight = jnp.exp(live - peak)
        own_weight = jnp.exp(own - peak)
        inverse = 1.0 / (jnp.sum(weight, axis=1, keepdims=True) + own_weight)
        weights[r] = (weight * inverse).astype(jnp.bfloat16)
        return (own_weight * inverse).astype(jnp.bfloat16).astype(jnp.float32)

    def mix(r, own_weight):
        mixed = jnp.dot(weights[r], vals[r], preferred_element_type=jnp.float32)
        o_f32[:, r, :] = mixed + own_weight * entries[r : r + 1, head_dim:]

    own_weights = []
    for r in range(min(2, req)):
        score(r)
    for r in range(req):
        own_weights.append(weigh(r))
        if r + 2 < req:
            score(r + 2)
        if r >= 1:
            mix(r - 1, own_weights[r - 1])
    mix(req - 1, own_weights[req - 1])
    for h in range(heads):
        att[:, h * head_dim : (h + 1) * head_dim] = o_f32[h].astype(jnp.bfloat16)
    att_out = pltpu.make_async_copy(att, att_ref, out_sem.at[1])
    att_out.start()
    place = acc.at[:, :, other]
    pltpu.make_async_remote_copy(
        src_ref=place, dst_ref=acc_rx, send_sem=acc_send.at[0], recv_sem=acc_recv.at[0],
        device_id={"wid": other}, device_id_type=MESH,
    ).wait_send()
    place = q_tx.at[:, pl.ds(0, hid_count - 1)]
    pltpu.make_async_remote_copy(
        src_ref=place, dst_ref=place, send_sem=q_send.at[0], recv_sem=q_recv.at[0],
        device_id={"hid": side}, device_id_type=MESH,
    ).wait_send()
    new_out.wait()
    att_out.wait()


def hand_on(att_ref, new_ref, att_out, new_out):
    att_out[...] = att_ref[...]
    new_out[...] = new_ref[...]


def body(
    tokens, norm_gain, query_weight, query_scale, kv_weight, kv_scale,
    keys_cache, values_cache, lengths,
):
    hid_count = lax.axis_size("hid")
    wid_count = lax.axis_size("wid")
    own_rows, half_width = tokens.shape
    local_cols = query_weight.shape[1]
    req, cache_len, head_dim = keys_cache.shape
    tiles = local_cols // head_dim
    heads = hid_count * tiles
    z_count = hid_count // ROWS_Y
    chunks = len(TWELFTHS)
    kv_cols = kv_weight.shape[1]
    bf16, f32 = jnp.bfloat16, jnp.float32
    dma = pltpu.SemaphoreType.DMA
    vm = pltpu.VMEM
    scratch = [
        vm((own_rows, half_width), bf16),
        vm((1, half_width), f32),
        vm((half_width, local_cols), bf16),
        vm((1, local_cols), f32),
        vm((half_width, kv_cols), bf16),
        vm((1, kv_cols), f32),
        vm(keys_cache.shape, bf16),
        vm(values_cache.shape, bf16),
        pltpu.SMEM(lengths.shape, jnp.int32),
        vm((hid_count, own_rows, half_width + LANES), bf16),
        vm((own_rows, 128), f32),
        vm((own_rows, 128), f32),
        vm((tiles, hid_count, wid_count, req, head_dim), f32),
        vm((tiles, hid_count, req, head_dim), f32),
        vm((wid_count, req, kv_cols), f32),
        vm((req, kv_cols), f32),
        vm((req, kv_cols), bf16),
        vm((tiles, hid_count, req, head_dim), bf16),
        vm((tiles, hid_count, req, head_dim), bf16),
        vm((heads, req, head_dim), f32),
        vm((heads, req, head_dim), f32),
        vm((req, heads, cache_len), f32),
        vm((req, heads, cache_len), bf16),
        vm((req, heads * head_dim), bf16),
        vm((hid_count, own_rows, TWELFTHS[0] * half_width // sum(TWELFTHS)), bf16),
        dma((9,)),
        dma((2, 2)),
        dma((3, z_count)),
        dma((2, z_count)),
        dma((z_count, chunks)),
        dma((chunks,)),
        dma((z_count,)),
        dma((1,)),
        dma((tiles,)),
        dma((1,)),
        dma((tiles,)),
        dma((2,)),
    ]
    hbm = pl.BlockSpec(memory_space=pl.ANY)
    attended, new_entries = pl.pallas_call(
        functools.partial(kernel, hid_count, wid_count),
        out_shape=(
            jax.ShapeDtypeStruct((req, heads * head_dim), bf16),
            jax.ShapeDtypeStruct((req, kv_cols), bf16),
        ),
        in_specs=[hbm] * 9,
        out_specs=(hbm, hbm),
        scratch_shapes=scratch,
        compiler_params=pltpu.CompilerParams(
            collective_id=0, has_side_effects=True, vmem_limit_bytes=60 * 1024 * 1024
        ),
    )(
        tokens, norm_gain.reshape(1, -1), query_weight, query_scale.reshape(1, -1),
        kv_weight, kv_scale.reshape(1, -1), keys_cache, values_cache, lengths,
    )
    whole = pl.BlockSpec(memory_space=pltpu.VMEM)
    return pl.pallas_call(
        hand_on,
        out_shape=(
            jax.ShapeDtypeStruct(attended.shape, bf16),
            jax.ShapeDtypeStruct(new_entries.shape, bf16),
        ),
        in_specs=[whole, whole],
        out_specs=(whole, whole),
    )(attended, new_entries)


def solution(mesh):
    placed = (
        P(("groups", "hid"), "wid"),
        P("wid"),
        P("wid", "hid"),
        P("hid"),
        P("wid", None),
        P(),
        P(("groups", "hid", "wid"), None, None),
        P(("groups", "hid", "wid"), None, None),
        P(("groups", "hid", "wid")),
    )
    return jax.shard_map(
        body,
        mesh=mesh,
        in_specs=placed,
        out_specs=(P(("groups", "hid", "wid"), None), P(("groups", "hid", "wid"), None)),
        check_vma=False,
    )
```
